32 devices in a mesh: row: 4 (over y, x), col: 4 (over z), depth: 2 (over core).
Axes of the slice: x: 2, y: 2, z: 4, core: 2. Of those that a mesh axis runs over, the one named last changes fastest.
Arguments:
- a_blocks: bfloat16 [32, 32, 2, 128, 128], P(('row', 'col', 'depth')), may hold values from -1.25 to 1.25
- a_columns: int32 [32, 32, 2], P(('row', 'col', 'depth')), may hold values from 0 to 319, as said below
- a_live: int32 [32, 32, 2], P(('row', 'col', 'depth')), may hold values from 0 to 1
- atom_rows: int32 [32], P(('row', 'col', 'depth')), may hold values from 0 to 31, as said below
- b_blocks: bfloat16 [320, 4, 6, 128, 128], P(('row', 'depth'), 'col'), may hold values from -1.25 to 1.25
- b_columns: int32 [320, 4, 6], P(('row', 'depth'), 'col'), may hold values from 0 to 319, as said below
- b_live: int32 [320, 4, 6], P(('row', 'depth'), 'col'), may hold values from 0 to 1, as said below
- c_columns: int32 [32, 4, 8], P('row', 'col'), may hold values from 0 to 319, as said below
- c_live: int32 [32, 4, 8], P('row', 'col'), may hold values from 0 to 1
Outputs:
- product: bfloat16 [32, 4, 8, 128, 128], P('row', 'col', 'depth')
The draws below stay inside these ranges and needn't reach their ends.
Inputs may be any that keep to these rules, and one draw needn't show every extreme that they name: `a_columns`: columns of one block row and group g are distinct and lie in g * 10 to (g + 1) * 10 - 1, also in empty slots. `atom_rows`: A permutation that maps every aligned run of 8 atom-order rows onto the same run of block rows. `b_columns`: columns of one block row and panel c are distinct and lie in c * 80 to (c + 1) * 80 - 1, also in empty slots. `b_live`: live slots of block row k hold columns within 16 of k, counted round. `c_columns`: columns of one block row and panel c are distinct and lie in c * 80 to (c + 1) * 80 - 1.
All inputs are finite; a program needn't handle non-finite values.
Results may differ from the reference program's by a relative error of at most 0.0043.
Values may be sent and summed in bfloat16 or wider, within the bound.
A program may use at most 320 MiB of HBM per device.

```python
import jax
import jax.numpy as jnp
from jax import lax

BS = 128
NB = 320
GW = 10
KR = 2
KBR = 6
KC = 8
R = 8
MB = 32
CW = 80
N_ROW = 4
N_COL = 4
N_DEPTH = 2


def distinct_pick(key, lead_shape, width, take):
    scores = jax.random.randint(key, lead_shape + (width,), 0, 1 << 20, dtype=jnp.int32)
    scores = scores * width + jnp.arange(width, dtype=jnp.int32)
    ordering = jnp.argsort(scores, axis=-1, stable=True)
    return ordering[..., :take].astype(jnp.int32)


def cycle_distance(first, second):
    gap = (first - second) % NB
    return jnp.minimum(gap, NB - gap)


def atom_order(key):
    run_count = MB // R
    ordering = distinct_pick(jax.random.fold_in(key, 13), (run_count,), R, R)
    return (ordering + (jnp.arange(run_count, dtype=jnp.int32) * R)[:, None]).reshape(MB)


def a_pattern(key):
    groups = NB // GW
    chosen = distinct_pick(jax.random.fold_in(key, 11), (MB, groups), GW, KR)
    columns = chosen + (jnp.arange(groups, dtype=jnp.int32) * GW)[None, :, None]
    block_row = atom_order(key)
    center = block_row * NB // MB
    group_middle = jnp.arange(groups, dtype=jnp.int32) * GW + GW // 2
    near = cycle_distance(group_middle[None, :], center[:, None]) <= 7 * GW
    favored = (center // GW)[:, None] == jnp.arange(groups, dtype=jnp.int32)[None, :]
    counts = jax.random.randint(jax.random.fold_in(key, 12), (MB, groups), 1, KR + 1, dtype=jnp.int32)
    far_counts = jax.random.randint(jax.random.fold_in(key, 18), (MB, groups), 0, KR + 1, dtype=jnp.int32)
    counts = jnp.where(favored, KR, jnp.where(near, counts, far_counts))
    live = (jnp.arange(KR, dtype=jnp.int32) < counts[..., None]).astype(jnp.int32)
    return (columns, live)


def b_pattern(key):
    panels = NB // CW
    noise = jax.random.randint(jax.random.fold_in(key, 14), (NB, panels, CW), 0, 1 << 16, dtype=jnp.int32)
    cells = jnp.arange(panels, dtype=jnp.int32)[:, None] * CW + jnp.arange(CW, dtype=jnp.int32)[None, :]
    near = cycle_distance(cells[None, :, :], jnp.arange(NB, dtype=jnp.int32)[:, None, None]) <= 16
    scores = (near.astype(jnp.int32) * (1 << 16) + noise) * CW + jnp.arange(CW, dtype=jnp.int32)
    order = jnp.argsort(-scores, axis=-1, stable=True)[..., :KBR].astype(jnp.int32)
    columns = order + (jnp.arange(panels, dtype=jnp.int32) * CW)[None, :, None]
    kept = jax.random.randint(jax.random.fold_in(key, 15), (NB, panels, KBR), 0, 4, dtype=jnp.int32)
    live = jnp.take_along_axis(near.astype(jnp.int32), order, axis=-1) * (kept > 0).astype(jnp.int32)
    return (columns, live)


def c_pattern(key):
    panels = NB // CW
    a_cols, a_flags = a_pattern(key)
    b_cols, b_flags = b_pattern(key)
    block_row = atom_order(key)
    positions = jnp.arange(NB, dtype=jnp.int32)
    a_hot = jnp.sum(((a_cols[..., None] == positions) & (a_flags[..., None] > 0)).astype(jnp.int32), axis=(1, 2))
    b_hot = jnp.sum(((b_cols[..., None] == positions) & (b_flags[..., None] > 0)).astype(jnp.int32), axis=(1, 2))
    reach_atom = jnp.dot(a_hot, b_hot, preferred_element_type=jnp.int32)
    inverse = jnp.zeros((MB,), jnp.int32).at[block_row].set(jnp.arange(MB, dtype=jnp.int32))
    reach = reach_atom[inverse].reshape(MB, panels, CW)
    noise = jax.random.randint(jax.random.fold_in(key, 16), (MB, panels, CW), 0, 1 << 12, dtype=jnp.int32)
    scores = (jnp.minimum(reach, 255) * (1 << 12) + noise) * CW + jnp.arange(CW, dtype=jnp.int32)
    order = jnp.argsort(-scores, axis=-1, stable=True)[..., :KC].astype(jnp.int32)
    columns = order + (jnp.arange(panels, dtype=jnp.int32) * CW)[None, :, None]
    reached = jnp.take_along_axis(reach, order, axis=-1)
    dropped = jax.random.randint(jax.random.fold_in(key, 17), (MB, panels, KC), 0, 8, dtype=jnp.int32)
    live = ((reached > 0) & (dropped > 0)).astype(jnp.int32)
    return (columns, live)


def draw_a_columns(key, part):
    return a_pattern(key)[0]


def draw_a_live(key, part):
    return a_pattern(key)[1]


def draw_atom_rows(key, part):
    return atom_order(key)


def draw_b_columns(key, part):
    return b_pattern(key)[0]


def draw_b_live(key, part):
    return b_pattern(key)[1]


def draw_c_columns(key, part):
    return c_pattern(key)[0]


def draw_c_live(key, part):
    return c_pattern(key)[1]


def block_scale(own_key, dims, split, smallest, largest):
    def one(axis_at, parts):
        draws = jax.random.uniform(jax.random.fold_in(jax.random.fold_in(own_key, 6), axis_at), (parts,), jnp.float32, smallest / len(split), largest / len(split))
        return jnp.repeat(jnp.exp(draws), dims[axis_at] // parts).reshape((-1,) + (1,) * (len(dims) - axis_at - 1))

    level = one(*split[0])
    for cut in split[1:]:
        level = level * one(*cut)
    return level


def normal_values(stream_key, shape, scale, limit, cuts=(), kind=jnp.bfloat16):
    entries = jax.random.normal(stream_key, shape, jnp.float32) * scale
    if len(cuts) > 0:
        entries = block_scale(stream_key, shape, cuts, -0.22, 0.18) * entries
    return jnp.clip(entries, min=-limit, max=limit).astype(kind)


def setup_inputs(seed: int = 0) -> dict:
    key_list = jax.random.split(jax.random.key(seed), 10)
    a_blocks = normal_values(key_list[0], (MB, NB // GW, KR, BS, BS), (0.7 * BS ** -0.25), 1.25, ((0, 32),))
    a_columns = draw_a_columns(jax.random.fold_in(key_list[9], 71), 0)
    a_live = draw_a_live(jax.random.fold_in(key_list[9], 71), 0)
    atom_rows = draw_atom_rows(jax.random.fold_in(key_list[9], 71), 0)
    b_blocks = normal_values(key_list[4], (NB, NB // CW, KBR, BS, BS), (0.7 * BS ** -0.25), 1.25, ((0, 8), (1, 4)))
    b_columns = draw_b_columns(jax.random.fold_in(key_list[9], 71), 0)
    b_live = draw_b_live(jax.random.fold_in(key_list[9], 71), 0)
    c_columns = draw_c_columns(jax.random.fold_in(key_list[9], 71), 0)
    c_live = draw_c_live(jax.random.fold_in(key_list[9], 71), 0)
    return {"a_blocks": a_blocks, "a_columns": a_columns, "a_live": a_live, "atom_rows": atom_rows, "b_blocks": b_blocks, "b_columns": b_columns, "b_live": b_live, "c_columns": c_columns, "c_live": c_live}


def reference(a_blocks, a_columns, a_live, atom_rows, b_blocks, b_columns, b_live, c_columns, c_live):
    stripe = NB // (N_ROW * N_DEPTH)
    panel_ids = jnp.arange(N_COL, dtype=jnp.int32)
    layer_ids = jnp.arange(N_DEPTH, dtype=jnp.int32)
    inverse = jnp.zeros((MB,), jnp.int32).at[atom_rows].set(jnp.arange(MB, dtype=jnp.int32))

    def one_row(target_row):
        source = inverse[target_row]
        block_tiles = a_blocks[source].reshape(-1, BS, BS)
        columns = a_columns[source].reshape(-1)
        live_flags = a_live[source].reshape(-1)
        found_columns = jnp.transpose(b_columns[columns], (1, 0, 2))
        found_live = jnp.transpose(b_live[columns], (1, 0, 2))
        wanted = c_columns[target_row]
        matched_pairs = (found_columns[:, None, :, :] == wanted[:, :, None, None]) & (found_live[:, None, :, :] > 0) & (live_flags[None, None, :, None] > 0)
        present = jnp.any(matched_pairs, axis=-1)
        slot_index = jnp.sum(jnp.where(matched_pairs, jnp.arange(KBR, dtype=jnp.int32), 0), axis=-1).astype(jnp.int32)
        selected_entries = b_blocks[columns[None, None, :], panel_ids[:, None, None], slot_index]
        selected_entries = jnp.where(present[..., None, None], selected_entries, jnp.zeros((), selected_entries.dtype))
        block_products = jnp.einsum('kqy,pckyt->pckqt', block_tiles.astype(jnp.float32), selected_entries.astype(jnp.float32))
        layer_of = (columns // stripe) % N_DEPTH
        selector = (layer_of[:, None] == layer_ids[None, :]).astype(jnp.float32)
        partial_sums = jnp.einsum('xuvae,vd->dxuae', block_products, selector)
        rounded = lax.optimization_barrier(partial_sums.astype(jnp.bfloat16))
        summed = jnp.sum(rounded.astype(jnp.float32), axis=0)
        summed = jnp.where(c_live[target_row][..., None, None] > 0, summed, jnp.float32(0.0))
        return summed.astype(jnp.bfloat16)

    return lax.map(one_row, jnp.arange(MB, dtype=jnp.int32))
```

```python
import functools

import jax
import jax.numpy as jnp
from jax import lax
from jax.experimental import pallas as pl
from jax.experimental.pallas import tpu as pltpu
from jax.sharding import PartitionSpec as P

GW = 10
REACH = 16
MESH = pl.DeviceIdType.MESH


def stripe_kinds(total, stripe, panel):
    kinds = {}
    for rel in range(total // stripe):
        groups = []
        for g in range(stripe // GW):
            first = rel * stripe + g * GW
            if any((k + REACH) % total < panel + 2 * REACH for k in range(first, first + GW)):
                groups.append(g)
        if groups:
            kinds[rel] = (groups[0], groups[-1] + 1)
    return kinds


def kernel(
    n_row, n_col, n_depth, kinds, slots,
    pick_ref, source_ref, keep_ref, a_ref, b_ref, out_ref,
    abuf, bbuf, cbuf, pbuf, b_sem, a_send, a_recv, c_send, c_recv,
):
    row, col, depth = (lax.axis_index(name) for name in ("row", "col", "depth"))
    stripes = n_row * n_depth
    per_panel = stripes // n_col
    run = n_col * n_depth
    me = (row * n_col + col) * n_depth + depth
    my_stripe = row * n_depth + depth
    my_rel = lax.rem(my_stripe - per_panel * col + stripes, stripes)
    rels = sorted(kinds)
    blocks = b_ref.shape[0]
    share = pbuf.shape[2]
    targets = share * n_depth
    width = a_ref.shape[0] // stripes
    groups = width // slots
    active = functools.reduce(jnp.logical_or, [my_rel == rel for rel in rels])

    def a_part(ref, rel):
        low, high = kinds[rel]
        return ref.at[pl.ds(low * slots, (high - low) * slots)]

    b_copy = pltpu.make_async_copy(b_ref, bbuf.at[pl.ds(0, blocks)], b_sem)

    @pl.when(active)
    def _():
        b_copy.start()

    sends = []
    for c in range(n_col):
        for rel in rels:
            s = (per_panel * c + rel) % stripes
            low, high = kinds[rel]
            src = a_ref.at[pl.ds(s * width + low * slots, (high - low) * slots)]
            mine = (my_stripe == s) & (col == c)
            index = len(sends)
            remote = pltpu.make_async_remote_copy(
                src_ref=src,
                dst_ref=a_part(abuf.at[me], rel),
                send_sem=a_send.at[index],
                recv_sem=a_recv.at[me],
                device_id=(s // n_depth, c, s % n_depth),
                device_id_type=MESH,
            )
            local = pltpu.make_async_copy(src, a_part(abuf.at[me], rel), a_recv.at[me])
            sends.append((mine, remote))

            @pl.when(mine)
            def _(local=local):
                local.start()

            @pl.when(jnp.logical_not(mine))
            def _(remote=remote):
                remote.start()

    for rel in rels:
        low, high = kinds[rel]
        gaps = [g for g in range(groups) if not low <= g < high]
        if gaps:

            @pl.when(my_rel == rel)
            def _(gaps=gaps):
                def clear(p, carry):
                    for g in gaps:
                        for v in range(g * slots, (g + 1) * slots):
                            abuf[p, v] = jnp.zeros(abuf.shape[2:], abuf.dtype)
                    return carry

                lax.fori_loop(0, abuf.shape[0], clear, 0)

    def share_copy(target_row, d, rel):
        return pltpu.make_async_remote_copy(
            src_ref=cbuf.at[target_row, d],
            dst_ref=pbuf.at[rels.index(rel)],
            send_sem=c_send.at[target_row, d],
            recv_sem=c_recv.at[rels.index(rel)],
            device_id=(target_row, col, d),
            device_id_type=MESH,
        )

    @pl.when(active)
    def _():
        b_copy.wait()
        bbuf[blocks] = jnp.zeros(bbuf.shape[1:], bbuf.dtype)

        def one_run(t, carry):
            target_row = lax.rem(row + t, n_row)

            def one_row(q, inner):
                p = target_row * run + q
                for rel in rels:

                    @pl.when(my_rel == rel)
                    def _(rel=rel):
                        part = a_part(abuf.at[p], rel)
                        pltpu.make_async_copy(part, part, a_recv.at[p]).wait()

                base = p * (width * targets)
                for u in range(0, targets, 2):
                    total = None
                    for v in range(0, width, 2):
                        left = jnp.concatenate([abuf[p, v], abuf[p, v + 1]], axis=1)
                        right = jnp.concatenate(
                            [
                                jnp.concatenate(
                                    [
                                        bbuf[pick_ref[base + (v + i) * targets + u]],
                                        bbuf[pick_ref[base + (v + i) * targets + u + 1]],
                                    ],
                                    axis=1,
                                )
                                for i in range(2)
                            ],
                            axis=0,
                        )
                        term = jnp.dot(left, right, preferred_element_type=jnp.float32)
                        total = term if total is None else total + term
                    edge = abuf.shape[-1]
                    for i in range(2):
                        cbuf[target_row, (u + i) // share, q, (u + i) % share] = total[
                            :, i * edge : (i + 1) * edge
                        ].astype(cbuf.dtype)
                return inner

            lax.fori_loop(0, run, one_row, 0)
            for d in range(n_depth):
                own = (t == 0) & (depth == d)
                for rel in rels:

                    @pl.when((my_rel == rel) & jnp.logical_not(own))
                    def _(d=d, rel=rel):
                        share_copy(target_row, d, rel).start()

                    @pl.when((my_rel == rel) & own)
                    def _(d=d, rel=rel):
                        slot = rels.index(rel)
                        pltpu.make_async_copy(
                            cbuf.at[target_row, d], pbuf.at[slot], c_recv.at[slot]
                        ).start()

            return carry

        lax.fori_loop(0, n_row, one_run, 0)

    for slot in range(len(rels)):
        pltpu.make_async_copy(pbuf.at[slot], pbuf.at[slot], c_recv.at[slot]).wait()

    def finish(i, carry):
        q = source_ref[i]
        for u in range(share):
            value = pbuf[0, q, u].astype(jnp.float32)
            for slot in range(1, len(rels)):
                value = value + pbuf[slot, q, u].astype(jnp.float32)
            kept = keep_ref[i * share + u] > 0
            out_ref[i, u] = jnp.where(kept, value, jnp.float32(0.0)).astype(out_ref.dtype)
        return carry

    lax.fori_loop(0, run, finish, 0)

    for mine, remote in sends:

        @pl.when(jnp.logical_not(mine))
        def _(remote=remote):
            remote.wait_send()

    @pl.when(active)
    def _():
        def settle(t, carry):
            target_row = lax.rem(row + t, n_row)
            for d in range(n_depth):

                @pl.when(jnp.logical_not((t == 0) & (depth == d)))
                def _(d=d):
                    share_copy(target_row, d, rels[0]).wait_send()

            return carry

        lax.fori_loop(0, n_row, settle, 0)


def on_device(
    a_blocks, a_columns, a_live, atom_rows, b_blocks, b_columns, b_live, c_columns, c_live
):
    n_row, n_col, n_depth = (lax.axis_size(name) for name in ("row", "col", "depth"))
    row, col, depth = (lax.axis_index(name) for name in ("row", "col", "depth"))
    _, group_count, slots = a_columns.shape
    edge = a_blocks.shape[-1]
    stripe, _, list_width = b_columns.shape
    run, _, targets = c_columns.shape
    stripes = n_row * n_depth
    total = stripe * stripes
    share = targets // n_depth
    width = group_count * slots // stripes
    row_count = n_row * run
    kinds = stripe_kinds(total, stripe, total // n_col)
    my_stripe = row * n_depth + depth

    packed = jnp.concatenate(
        [
            jnp.where(a_live > 0, a_columns, -1).reshape(1, -1),
            c_columns.reshape(1, -1),
            jnp.broadcast_to(atom_rows.reshape(1, 1), (1, 128)),
        ],
        axis=1,
    )
    everyone = lax.all_gather(packed, ("row", "col", "depth"), axis=0, tiled=True)
    slot_count = group_count * slots
    a_keys = lax.dynamic_slice_in_dim(everyone[:, :slot_count], my_stripe * width, width, 1)
    panel_lists = everyone[:, slot_count : slot_count + run * targets].reshape(
        n_row, n_col, n_depth, run, targets
    )[:, :, 0]
    panel_lists = lax.dynamic_index_in_dim(panel_lists, col, 1, keepdims=False)
    atoms = everyone[:, slot_count + run * targets]
    hot = atoms[:, None] == jnp.arange(row_count, dtype=jnp.int32)
    wanted = jnp.sum(
        jnp.where(hot[:, :, None], panel_lists.reshape(1, row_count, targets), 0), axis=1
    )
    block_count = stripe * list_width
    b_keys = jnp.where(b_live > 0, b_columns, -1).reshape(-1)
    numbers = jnp.arange(block_count, dtype=jnp.int32)
    same_row = (a_keys - my_stripe * stripe)[:, :, None] == numbers // list_width
    same_column = wanted[:, :, None] == b_keys
    picks = block_count + jnp.sum(
        jnp.where(
            same_row[:, :, None, :] & same_column[:, None, :, :], numbers - block_count, 0
        ),
        axis=-1,
    )
    own_atoms = lax.dynamic_slice_in_dim(atoms, row * run, run, 0) - row * run
    places = jnp.arange(run, dtype=jnp.int32)
    source = jnp.sum(jnp.where(own_atoms[None, :] == places[:, None], places[None, :], 0), axis=1)
    keep = lax.dynamic_slice_in_dim(c_live[:, 0, :], depth * share, share, 1).reshape(-1)

    copies = n_col * len(kinds)
    result = pl.pallas_call(
        functools.partial(kernel, n_row, n_col, n_depth, kinds, slots),
        out_shape=jax.ShapeDtypeStruct((run, share, edge, edge), jnp.bfloat16),
        in_specs=[pl.BlockSpec(memory_space=pltpu.SMEM)] * 3
        + [pl.BlockSpec(memory_space=pl.ANY)] * 2,
        out_specs=pl.BlockSpec(memory_space=pltpu.VMEM),
        scratch_shapes=[
            pltpu.VMEM((row_count, width, edge, edge), jnp.bfloat16),
            pltpu.VMEM((block_count + 1, edge, edge), jnp.bfloat16),
            pltpu.VMEM((n_row, n_depth, run, share, edge, edge), jnp.bfloat16),
            pltpu.VMEM((len(kinds), run, share, edge, edge), jnp.bfloat16),
            pltpu.SemaphoreType.DMA,
            pltpu.SemaphoreType.DMA((copies,)),
            pltpu.SemaphoreType.DMA((row_count,)),
            pltpu.SemaphoreType.DMA((n_row, n_depth)),
            pltpu.SemaphoreType.DMA((len(kinds),)),
        ],
        compiler_params=pltpu.CompilerParams(
            has_side_effects=True, vmem_limit_bytes=60 * 1024 * 1024
        ),
    )(
        picks.reshape(-1),
        source,
        keep,
        a_blocks.reshape(-1, edge, edge),
        b_blocks.reshape(-1, edge, edge),
    )
    return result[:, None]


def solution(mesh):
    placed = (
        P(("row", "col", "depth"), None, None, None, None),
        P(("row", "col", "depth"), None, None),
        P(("row", "col", "depth"), None, None),
        P(("row", "col", "depth")),
        P(("row", "depth"), "col", None, None, None),
        P(("row", "depth"), "col", None),
        P(("row", "depth"), "col", None),
        P("row", "col", None),
        P("row", "col", None),
    )
    return jax.shard_map(
        on_device,
        mesh=mesh,
        in_specs=placed,
        out_specs=P("row", "col", "depth", None, None),
        check_vma=False,
    )
```

```python
import functools

import jax
import jax.numpy as jnp
from jax import lax
from jax.experimental import pallas as pl
from jax.experimental.pallas import tpu as pltpu
from jax.sharding import PartitionSpec as P

GW = 10
REACH = 16
MESH = pl.DeviceIdType.MESH


def stripe_kinds(total, stripe, panel):
    kinds = {}
    for rel in range(total // stripe):
        groups = []
        for g in range(stripe // GW):
            first = rel * stripe + g * GW
            if any((k + REACH) % total < panel + 2 * REACH for k in range(first, first + GW)):
                groups.append(g)
        if groups:
            kinds[rel] = (groups[0], groups[-1] + 1)
    return kinds


def kernel(
    n_row, n_col, n_depth, kinds, slots,
    pack_ref, keys_ref, keep_ref, a_ref, b_ref, out_ref,
    lbuf, picks, pick_s, abuf, bbuf, cbuf, mbuf, pbuf,
    l_send, l_recv, s_sem, b_sem, a_send, a_recv, m_send, m_recv, m_free, c_send, c_recv,
):
    row, col, depth = (lax.axis_index(name) for name in ("row", "col", "depth"))
    stripes = n_row * n_depth
    per_panel = stripes // n_col
    run = n_col * n_depth
    rows = n_row * run
    me = (row * n_col + col) * n_depth + depth
    my_stripe = row * n_depth + depth
    my_rel = lax.rem(my_stripe - per_panel * col + stripes, stripes)
    rels = sorted(kinds)
    blocks = b_ref.shape[0]
    share = pbuf.shape[2]
    targets = share * n_depth
    width = a_ref.shape[0] // stripes
    groups = width // slots
    active = functools.reduce(jnp.logical_or, [my_rel == rel for rel in rels])
    paired = [rel for rel in rels if rel ^ 1 in kinds and n_depth == 2]
    lone = [rel for rel in rels if rel not in paired]
    senders = sorted({rel // 2 * 2 if rel in paired else rel for rel in rels})

    def sender(rel):
        return senders.index(rel // 2 * 2 if rel in paired else rel)

    def a_part(ref, rel):
        low, high = kinds[rel]
        return ref.at[pl.ds(low * slots, (high - low) * slots)]

    def list_copy(offset):
        dest = lax.rem(me + offset, rows)
        dest_row, dest_col, dest_depth = dest // run, dest // n_depth % n_col, dest % n_depth
        return pltpu.make_async_remote_copy(
            src_ref=pack_ref.at[dest_row * n_depth + dest_depth],
            dst_ref=lbuf.at[me],
            send_sem=l_send,
            recv_sem=l_recv,
            device_id=(dest_row, dest_col, dest_depth),
            device_id_type=MESH,
        )

    pltpu.make_async_copy(pack_ref.at[my_stripe], lbuf.at[me], l_recv).start()

    def send_list(offset, carry):
        list_copy(offset).start()
        return carry

    lax.fori_loop(1, rows, send_list, 0)

    b_copy = pltpu.make_async_copy(b_ref, bbuf.at[pl.ds(0, blocks)], b_sem)

    @pl.when(active)
    def _():
        b_copy.start()

    sends = []
    for t in range(n_col):
        c = lax.rem(row + t, n_col)
        for rel in rels:
            s = lax.rem(per_panel * c + rel, stripes)
            low, high = kinds[rel]
            src = a_ref.at[pl.ds(s * width + low * slots, (high - low) * slots)]
            mine = (my_stripe == s) & (col == c)
            remote = pltpu.make_async_remote_copy(
                src_ref=src,
                dst_ref=a_part(abuf.at[me], rel),
                send_sem=a_send.at[len(sends)],
                recv_sem=a_recv.at[me],
                device_id=(s // n_depth, c, s % n_depth),
                device_id_type=MESH,
            )
            local = pltpu.make_async_copy(src, a_part(abuf.at[me], rel), a_recv.at[me])
            sends.append((mine, remote))

            @pl.when(mine)
            def _(local=local):
                local.start()

            @pl.when(jnp.logical_not(mine))
            def _(remote=remote):
                remote.start()

    for rel in rels:
        low, high = kinds[rel]
        gaps = [g for g in range(groups) if not low <= g < high]
        if gaps:

            @pl.when(my_rel == rel)
            def _(gaps=gaps):
                def clear(p, carry):
                    for g in gaps:
                        for v in range(g * slots, (g + 1) * slots):
                            abuf[p, v] = jnp.zeros(abuf.shape[2:], abuf.dtype)
                    return carry

                lax.fori_loop(0, rows, clear, 0)

    pltpu.make_async_copy(lbuf, lbuf, l_recv).wait()
    lanes = lbuf.shape[2]

    def match(p, carry):
        column_row = lbuf[p, 0:1, :]
        place = lbuf[p, 1:2, :]
        table = lbuf[(p // run * n_col + col) * n_depth, 8:, :]
        at = lax.broadcasted_iota(jnp.int32, (run, lanes), 0)
        wanted = jnp.sum(jnp.where(at == place, table, 0), axis=0, keepdims=True)
        hit = (keys_ref[1] == column_row) & (keys_ref[0] == wanted)
        number = lax.broadcasted_iota(jnp.int32, (blocks, lanes), 0)
        picks[pl.ds(p, 1), :] = jnp.min(
            jnp.where(hit, number, blocks), axis=0, keepdims=True
        )
        return carry

    lax.fori_loop(0, rows, match, 0)
    for q in range(run):
        picks[pl.ds(rows + q, 1), :] = lbuf[row * run + q, 1:2, :]
    to_scalars = pltpu.make_async_copy(picks, pick_s, s_sem)
    to_scalars.start()
    to_scalars.wait()

    def share_copy(target_row, d, slot):
        return pltpu.make_async_remote_copy(
            src_ref=cbuf.at[target_row, d],
            dst_ref=pbuf.at[slot],
            send_sem=c_send.at[target_row, d],
            recv_sem=c_recv.at[slot],
            device_id=(target_row, col, d),
            device_id_type=MESH,
        )

    def start_share(target_row, d, slot):
        own = (target_row == row) & (depth == d)

        @pl.when(jnp.logical_not(own))
        def _():
            share_copy(target_row, d, slot).start()

        @pl.when(own)
        def _():
            pltpu.make_async_copy(cbuf.at[target_row, d], pbuf.at[slot], c_recv.at[slot]).start()

    def settle_share(target_row, d):
        @pl.when(jnp.logical_not((target_row == row) & (depth == d)))
        def _():
            share_copy(target_row, d, 0).wait_send()

    is_paired = functools.reduce(jnp.logical_or, [my_rel == rel for rel in paired], False)

    def mate_copy(t, target_row):
        return pltpu.make_async_remote_copy(
            src_ref=cbuf.at[target_row, 1 - depth],
            dst_ref=mbuf.at[t % 2],
            send_sem=m_send.at[t % 2],
            recv_sem=m_recv.at[t % 2],
            device_id=(row, col, 1 - depth),
            device_id_type=MESH,
        )

    @pl.when(active)
    def _():
        b_copy.wait()
        bbuf[blocks] = jnp.zeros(bbuf.shape[1:], bbuf.dtype)

        def one_run(t, carry):
            target_row = lax.rem(col - t + n_row * n_col, n_row)

            def one_row(q, inner):
                p = target_row * run + q
                for rel in rels:

                    @pl.when(my_rel == rel)
                    def _(rel=rel):
                        part = a_part(abuf.at[p], rel)
                        pltpu.make_async_copy(part, part, a_recv.at[p]).wait()

                for u in range(0, targets, 2):
                    total = None
                    for v in range(0, width, 2):
                        left = jnp.concatenate([abuf[p, v], abuf[p, v + 1]], axis=1)
                        right = jnp.concatenate(
                            [
                                jnp.concatenate(
                                    [
                                        bbuf[pick_s[p, (v + i) * targets + u]],
                                        bbuf[pick_s[p, (v + i) * targets + u + 1]],
                                    ],
                                    axis=1,
                                )
                                for i in range(2)
                            ],
                            axis=0,
                        )
                        term = jnp.dot(left, right, preferred_element_type=jnp.float32)
                        total = term if total is None else total + term
                    edge = abuf.shape[-1]
                    for i in range(2):
                        cbuf[target_row, (u + i) // share, q, (u + i) % share] = total[
                            :, i * edge : (i + 1) * edge
                        ].astype(cbuf.dtype)
                return inner

            lax.fori_loop(0, run, one_row, 0)
            for rel in lone:

                @pl.when(my_rel == rel)
                def _(rel=rel):
                    for d in range(n_depth):
                        start_share(target_row, d, sender(rel))

            if paired:

                @pl.when(is_paired)
                def _():
                    @pl.when(t >= 2)
                    def _():
                        pl.semaphore_wait(m_free, 1)

                    exchange = mate_copy(t, target_row)
                    exchange.start()
                    exchange.wait()

                    def merge(q, inner):
                        for u in range(share):
                            cbuf[target_row, depth, q, u] = (
                                cbuf[target_row, depth, q, u].astype(jnp.float32)
                                + mbuf[t % 2, q, u].astype(jnp.float32)
                            ).astype(cbuf.dtype)
                        return inner

                    lax.fori_loop(0, run, merge, 0)

                    @pl.when(t < n_row - 2)
                    def _():
                        pl.semaphore_signal(
                            m_free,
                            inc=1,
                            device_id=(row, col, 1 - depth),
                            device_id_type=MESH,
                        )

                for slot, first in enumerate(senders):
                    if first in paired:

                        @pl.when(my_rel // 2 * 2 == first)
                        def _(slot=slot):
                            start_share(target_row, depth, slot)

            return carry

        lax.fori_loop(0, n_row, one_run, 0)

    for slot in range(len(senders)):
        pltpu.make_async_copy(pbuf.at[slot], pbuf.at[slot], c_recv.at[slot]).wait()

    def finish(i, carry):
        q = jnp.int32(0)
        for j in range(run):
            q = jnp.where(pick_s[rows + j, 0] == i, j, q)
        for u in range(share):
            value = pbuf[0, q, u].astype(jnp.float32)
            for slot in range(1, len(senders)):
                value = value + pbuf[slot, q, u].astype(jnp.float32)
            kept = keep_ref[i * share + u] > 0
            out_ref[i, u] = jnp.where(kept, value, jnp.float32(0.0)).astype(out_ref.dtype)
        return carry

    lax.fori_loop(0, run, finish, 0)

    sent = lbuf.at[pl.ds(0, rows - 1)]
    pltpu.make_async_copy(sent, sent, l_send).wait()
    for mine, remote in sends:

        @pl.when(jnp.logical_not(mine))
        def _(remote=remote):
            remote.wait_send()

    def settle(target_row, carry):
        for rel in lone:

            @pl.when(my_rel == rel)
            def _():
                for d in range(n_depth):
                    settle_share(target_row, d)

        if paired:

            @pl.when(is_paired)
            def _():
                settle_share(target_row, depth)

        return carry

    lax.fori_loop(0, n_row, settle, 0)


def on_device(
    a_blocks, a_columns, a_live, atom_rows, b_blocks, b_columns, b_live, c_columns, c_live
):
    n_row, n_col, n_depth = (lax.axis_size(name) for name in ("row", "col", "depth"))
    row, depth = (lax.axis_index(name) for name in ("row", "depth"))
    _, group_count, slots = a_columns.shape
    edge = a_blocks.shape[-1]
    stripe, _, list_width = b_columns.shape
    run, _, targets = c_columns.shape
    stripes = n_row * n_depth
    total = stripe * stripes
    share = targets // n_depth
    width = group_count * slots // stripes
    row_count = n_row * run
    kinds = stripe_kinds(total, stripe, total // n_col)
    senders = {rel // 2 * 2 if rel ^ 1 in kinds and n_depth == 2 else rel for rel in kinds}
    block_count = stripe * list_width
    lanes = -(-width * targets // 128) * 128
    spare = lanes - width * targets

    firsts = jnp.arange(stripes, dtype=jnp.int32)[:, None] * stripe
    a_keys = jnp.where(a_live > 0, a_columns, -total).reshape(stripes, width) - firsts
    a_keys = jnp.repeat(a_keys, targets, axis=1)
    a_keys = jnp.pad(a_keys, ((0, 0), (0, spare)), constant_values=-1)[:, None]
    place = jnp.broadcast_to((atom_rows - row * run).reshape(1, 1, 1), (stripes, 1, lanes))
    table = jnp.tile(c_columns[:, 0, :], (1, width))
    table = jnp.pad(table, ((0, 0), (0, spare)), constant_values=-2)
    pack = jnp.concatenate(
        [
            a_keys,
            place,
            jnp.zeros((stripes, 6, lanes), jnp.int32),
            jnp.broadcast_to(table[None], (stripes, run, lanes)),
        ],
        axis=1,
    )
    b_keys = jnp.where(b_live > 0, b_columns, -1).reshape(-1)
    b_rows = jnp.arange(block_count, dtype=jnp.int32) // list_width
    keys = jnp.broadcast_to(jnp.stack([b_keys, b_rows])[:, :, None], (2, block_count, lanes))
    keep = lax.dynamic_slice_in_dim(c_live[:, 0, :], depth * share, share, 1).reshape(-1)

    copies = n_col * len(kinds)
    result = pl.pallas_call(
        functools.partial(kernel, n_row, n_col, n_depth, kinds, slots),
        out_shape=jax.ShapeDtypeStruct((run, share, edge, edge), jnp.bfloat16),
        in_specs=[
            pl.BlockSpec(memory_space=pltpu.VMEM),
            pl.BlockSpec(memory_space=pltpu.VMEM),
            pl.BlockSpec(memory_space=pltpu.SMEM),
            pl.BlockSpec(memory_space=pl.ANY),
            pl.BlockSpec(memory_space=pl.ANY),
        ],
        out_specs=pl.BlockSpec(memory_space=pltpu.VMEM),
        scratch_shapes=[
            pltpu.VMEM((row_count, 8 + run, lanes), jnp.int32),
            pltpu.VMEM((row_count + run, lanes), jnp.int32),
            pltpu.SMEM((row_count + run, lanes), jnp.int32),
            pltpu.VMEM((row_count, width, edge, edge), jnp.bfloat16),
            pltpu.VMEM((block_count + 1, edge, edge), jnp.bfloat16),
            pltpu.VMEM((n_row, n_depth, run, share, edge, edge), jnp.bfloat16),
            pltpu.VMEM((2, run, share, edge, edge), jnp.bfloat16),
            pltpu.VMEM((len(senders), run, share, edge, edge), jnp.bfloat16),
            pltpu.SemaphoreType.DMA,
            pltpu.SemaphoreType.DMA,
            pltpu.SemaphoreType.DMA,
            pltpu.SemaphoreType.DMA,
            pltpu.SemaphoreType.DMA((copies,)),
            pltpu.SemaphoreType.DMA((row_count,)),
            pltpu.SemaphoreType.DMA((2,)),
            pltpu.SemaphoreType.DMA((2,)),
            pltpu.SemaphoreType.REGULAR,
            pltpu.SemaphoreType.DMA((n_row, n_depth)),
            pltpu.SemaphoreType.DMA((len(senders),)),
        ],
        compiler_params=pltpu.CompilerParams(
            has_side_effects=True, vmem_limit_bytes=60 * 1024 * 1024
        ),
    )(
        pack,
        keys,
        keep,
        a_blocks.reshape(-1, edge, edge),
        b_blocks.reshape(-1, edge, edge),
    )
    return result[:, None]


def solution(mesh):
    placed = (
        P(("row", "col", "depth"), None, None, None, None),
        P(("row", "col", "depth"), None, None),
        P(("row", "col", "depth"), None, None),
        P(("row", "col", "depth")),
        P(("row", "depth"), "col", None, None, None),
        P(("row", "depth"), "col", None),
        P(("row", "depth"), "col", None),
        P("row", "col", None),
        P("row", "col", None),
    )
    return jax.shard_map(
        on_device,
        mesh=mesh,
        in_specs=placed,
        out_specs=P("row", "col", "depth", None, None),
        check_vma=False,
    )
```

```python
import functools

import jax
import jax.numpy as jnp
from jax import lax
from jax.experimental import pallas as pl
from jax.experimental.pallas import tpu as pltpu
from jax.sharding import PartitionSpec as P

GW = 10
REACH = 16
MESH = pl.DeviceIdType.MESH


def stripe_kinds(total, stripe, panel):
    kinds = {}
    for rel in range(total // stripe):
        groups = []
        for g in range(stripe // GW):
            first = rel * stripe + g * GW
            if any((k + REACH) % total < panel + 2 * REACH for k in range(first, first + GW)):
                groups.append(g)
        if groups:
            kinds[rel] = (groups[0], groups[-1] + 1)
    return kinds


def flip(index, step, count):
    return lax.rem(index // 2 + step // 2, count // 2) * 2 + lax.rem(index + step, 2)


def kernel(
    n_row, n_col, n_depth, kinds, slots,
    pack_ref, keys_ref, keep_ref, a_ref, b_ref, out_ref,
    lbuf, picks, pick_s, abuf, bbuf, cbuf, mbuf, pbuf,
    rbuf, r_recv, f_send,
    l_send, l_recv, s_sem, b_sem, a_send, a_recv, m_send, m_recv, m_free, c_send, c_recv,
):
    row, col, depth = (lax.axis_index(name) for name in ("row", "col", "depth"))
    stripes = n_row * n_depth
    per_panel = stripes // n_col
    run = n_col * n_depth
    rows = n_row * run
    me = (row * n_col + col) * n_depth + depth
    my_stripe = row * n_depth + depth
    my_rel = lax.rem(my_stripe - per_panel * col + stripes, stripes)
    rels = sorted(kinds)
    blocks = b_ref.shape[0]
    share = pbuf.shape[2]
    targets = share * n_depth
    width = a_ref.shape[0] // stripes
    groups = width // slots
    active = functools.reduce(jnp.logical_or, [my_rel == rel for rel in rels])
    paired = [rel for rel in rels if rel ^ 1 in kinds and n_depth == 2]
    lone = [rel for rel in rels if rel not in paired]
    senders = sorted({rel // 2 * 2 if rel in paired else rel for rel in rels})

    relayed = (n_row, n_col, n_depth) == (4, 4, 2) and sorted(kinds) == [0, 1, 2, 7]

    def sender(rel):
        return senders.index(rel // 2 * 2 if rel in paired else rel)

    def a_part(ref, rel):
        low, high = kinds[rel]
        return ref.at[pl.ds(low * slots, (high - low) * slots)]

    def list_copy(offset):
        dest = lax.rem(me + offset, rows)
        dest_row, dest_col, dest_depth = dest // run, dest // n_depth % n_col, dest % n_depth
        return pltpu.make_async_remote_copy(
            src_ref=pack_ref.at[dest_row * n_depth + dest_depth],
            dst_ref=lbuf.at[me],
            send_sem=l_send,
            recv_sem=l_recv,
            device_id=(dest_row, dest_col, dest_depth),
            device_id_type=MESH,
        )

    pltpu.make_async_copy(pack_ref.at[my_stripe], lbuf.at[me], l_recv).start()

    def send_list(offset, carry):
        list_copy(offset).start()
        return carry

    lax.fori_loop(1, rows, send_list, 0)

    b_copy = pltpu.make_async_copy(b_ref, bbuf.at[pl.ds(0, blocks)], b_sem)

    @pl.when(active)
    def _():
        b_copy.start()

    sends = []
    for t in reversed(range(n_col)):
        c = flip(row, t, n_col)
        for rel in rels:
            s = lax.rem(per_panel * c + rel, stripes)
            low, high = kinds[rel]
            src = a_ref.at[pl.ds(s * width + low * slots, (high - low) * slots)]
            if relayed and t == 3 and rel == 1:
                place = col * n_depth + depth
                remote = pltpu.make_async_remote_copy(
                    src_ref=src,
                    dst_ref=rbuf.at[place],
                    send_sem=a_send.at[len(sends)],
                    recv_sem=r_recv.at[place],
                    device_id=(flip(c, 1, n_row), c, 1 - lax.rem(c, 2)),
                    device_id_type=MESH,
                )
                remote.start()
                sends.append((False, remote))
                continue
            mine = (my_stripe == s) & (col == c)
            remote = pltpu.make_async_remote_copy(
                src_ref=src,
                dst_ref=a_part(abuf.at[me], rel),
                send_sem=a_send.at[len(sends)],
                recv_sem=a_recv.at[me],
                device_id=(s // n_depth, c, s % n_depth),
                device_id_type=MESH,
            )
            local = pltpu.make_async_copy(src, a_part(abuf.at[me], rel), a_recv.at[me])
            sends.append((mine, remote))

            @pl.when(mine)
            def _(local=local):
                local.start()

            @pl.when(jnp.logical_not(mine))
            def _(remote=remote):
                remote.start()

    forwards = (row == flip(col, 1, n_row)) & (depth == 1 - lax.rem(col, 2))

    def forward_copy(q):
        p = flip(col, 3, n_row) * run + q
        return pltpu.make_async_remote_copy(
            src_ref=rbuf.at[q],
            dst_ref=abuf.at[p],
            send_sem=f_send,
            recv_sem=a_recv.at[p],
            device_id=(col, col, 1),
            device_id_type=MESH,
        )

    if relayed:

        @pl.when(forwards)
        def _():
            def forward(q, carry):
                pltpu.make_async_copy(rbuf.at[q], rbuf.at[q], r_recv.at[q]).wait()
                forward_copy(q).start()
                return carry

            lax.fori_loop(0, run, forward, 0)

    for rel in rels:
        low, high = kinds[rel]
        gaps = [g for g in range(groups) if not low <= g < high]
        if gaps:

            @pl.when(my_rel == rel)
            def _(gaps=gaps):
                def clear(p, carry):
                    for g in gaps:
                        for v in range(g * slots, (g + 1) * slots):
                            abuf[p, v] = jnp.zeros(abuf.shape[2:], abuf.dtype)
                    return carry

                lax.fori_loop(0, rows, clear, 0)

    pltpu.make_async_copy(lbuf, lbuf, l_recv).wait()
    lanes = lbuf.shape[2]

    def match(p, carry):
        column_row = lbuf[p, 0:1, :]
        place = lbuf[p, 1:2, :]
        table = lbuf[(p // run * n_col + col) * n_depth, 8:, :]
        at = lax.broadcasted_iota(jnp.int32, (run, lanes), 0)
        wanted = jnp.sum(jnp.where(at == place, table, 0), axis=0, keepdims=True)
        hit = (keys_ref[1] == column_row) & (keys_ref[0] == wanted)
        number = lax.broadcasted_iota(jnp.int32, (blocks, lanes), 0)
        picks[pl.ds(p, 1), :] = jnp.min(
            jnp.where(hit, number, blocks), axis=0, keepdims=True
        )
        return carry

    lax.fori_loop(0, rows, match, 0)
    for q in range(run):
        picks[pl.ds(rows + q, 1), :] = lbuf[row * run + q, 1:2, :]
    to_scalars = pltpu.make_async_copy(picks, pick_s, s_sem)
    to_scalars.start()
    to_scalars.wait()

    def share_copy(target_row, d, slot):
        return pltpu.make_async_remote_copy(
            src_ref=cbuf.at[target_row, d],
            dst_ref=pbuf.at[slot],
            send_sem=c_send.at[target_row, d],
            recv_sem=c_recv.at[slot],
            device_id=(target_row, col, d),
            device_id_type=MESH,
        )

    def start_share(target_row, d, slot):
        own = (target_row == row) & (depth == d)

        @pl.when(jnp.logical_not(own))
        def _():
            share_copy(target_row, d, slot).start()

        @pl.when(own)
        def _():
            pltpu.make_async_copy(cbuf.at[target_row, d], pbuf.at[slot], c_recv.at[slot]).start()

    def settle_share(target_row, d):
        @pl.when(jnp.logical_not((target_row == row) & (depth == d)))
        def _():
            share_copy(target_row, d, 0).wait_send()

    is_paired = functools.reduce(jnp.logical_or, [my_rel == rel for rel in paired], False)

    def mate_copy(t, target_row):
        return pltpu.make_async_remote_copy(
            src_ref=cbuf.at[target_row, 1 - depth],
            dst_ref=mbuf.at[t % 2],
            send_sem=m_send.at[t % 2],
            recv_sem=m_recv.at[t % 2],
            device_id=(row, col, 1 - depth),
            device_id_type=MESH,
        )

    @pl.when(active)
    def _():
        b_copy.wait()
        bbuf[blocks] = jnp.zeros(bbuf.shape[1:], bbuf.dtype)

        def one_run(t, carry):
            target_row = flip(col, n_row - 1 - t, n_row)

            def one_row(q, inner):
                p = target_row * run + q
                for rel in rels:

                    @pl.when(my_rel == rel)
                    def _(rel=rel):
                        part = a_part(abuf.at[p], rel)
                        pltpu.make_async_copy(part, part, a_recv.at[p]).wait()

                for u in range(0, targets, 2):
                    total = None
                    for v in range(0, width, 2):
                        left = jnp.concatenate([abuf[p, v], abuf[p, v + 1]], axis=1)
                        right = jnp.concatenate(
                            [
                                jnp.concatenate(
                                    [
                                        bbuf[pick_s[p, (v + i) * targets + u]],
                                        bbuf[pick_s[p, (v + i) * targets + u + 1]],
                                    ],
                                    axis=1,
                                )
                                for i in range(2)
                            ],
                            axis=0,
                        )
                        term = jnp.dot(left, right, preferred_element_type=jnp.float32)
                        total = term if total is None else total + term
                    edge = abuf.shape[-1]
                    for i in range(2):
                        cbuf[target_row, (u + i) // share, q, (u + i) % share] = total[
                            :, i * edge : (i + 1) * edge
                        ].astype(cbuf.dtype)
                return inner

            lax.fori_loop(0, run, one_row, 0)
            for rel in lone:

                @pl.when(my_rel == rel)
                def _(rel=rel):
                    for d in range(n_depth):
                        start_share(target_row, d, sender(rel))

            if paired:

                @pl.when(is_paired)
                def _():
                    @pl.when(t >= 2)
                    def _():
                        pl.semaphore_wait(m_free, 1)

                    exchange = mate_copy(t, target_row)
                    exchange.start()
                    exchange.wait()

                    def merge(q, inner):
                        for u in range(share):
                            cbuf[target_row, depth, q, u] = (
                                cbuf[target_row, depth, q, u].astype(jnp.float32)
                                + mbuf[t % 2, q, u].astype(jnp.float32)
                            ).astype(cbuf.dtype)
                        return inner

                    lax.fori_loop(0, run, merge, 0)

                    @pl.when(t < n_row - 2)
                    def _():
                        pl.semaphore_signal(
                            m_free,
                            inc=1,
                            device_id=(row, col, 1 - depth),
                            device_id_type=MESH,
                        )

                for slot, first in enumerate(senders):
                    if first in paired:

                        @pl.when(my_rel // 2 * 2 == first)
                        def _(slot=slot):
                            start_share(target_row, depth, slot)

            return carry

        lax.fori_loop(0, n_row, one_run, 0)

    for slot in range(len(senders)):
        pltpu.make_async_copy(pbuf.at[slot], pbuf.at[slot], c_recv.at[slot]).wait()

    def finish(i, carry):
        q = jnp.int32(0)
        for j in range(run):
            q = jnp.where(pick_s[rows + j, 0] == i, j, q)
        for u in range(share):
            value = pbuf[0, q, u].astype(jnp.float32)
            for slot in range(1, len(senders)):
                value = value + pbuf[slot, q, u].astype(jnp.float32)
            kept = keep_ref[i * share + u] > 0
            out_ref[i, u] = jnp.where(kept, value, jnp.float32(0.0)).astype(out_ref.dtype)
        return carry

    lax.fori_loop(0, run, finish, 0)

    sent = lbuf.at[pl.ds(0, rows - 1)]
    pltpu.make_async_copy(sent, sent, l_send).wait()
    if relayed:

        @pl.when(forwards)
        def _():
            pltpu.make_async_copy(rbuf, rbuf, f_send).wait()

    for mine, remote in sends:
        if mine is False:
            remote.wait_send()
            continue

        @pl.when(jnp.logical_not(mine))
        def _(remote=remote):
            remote.wait_send()

    def settle(target_row, carry):
        for rel in lone:

            @pl.when(my_rel == rel)
            def _():
                for d in range(n_depth):
                    settle_share(target_row, d)

        if paired:

            @pl.when(is_paired)
            def _():
                settle_share(target_row, depth)

        return carry

    lax.fori_loop(0, n_row, settle, 0)


def on_device(
    a_blocks, a_columns, a_live, atom_rows, b_blocks, b_columns, b_live, c_columns, c_live
):
    n_row, n_col, n_depth = (lax.axis_size(name) for name in ("row", "col", "depth"))
    row, depth = (lax.axis_index(name) for name in ("row", "depth"))
    _, group_count, slots = a_columns.shape
    edge = a_blocks.shape[-1]
    stripe, _, list_width = b_columns.shape
    run, _, targets = c_columns.shape
    stripes = n_row * n_depth
    total = stripe * stripes
    share = targets // n_depth
    width = group_count * slots // stripes
    row_count = n_row * run
    kinds = stripe_kinds(total, stripe, total // n_col)
    senders = {rel // 2 * 2 if rel ^ 1 in kinds and n_depth == 2 else rel for rel in kinds}
    block_count = stripe * list_width
    lanes = -(-width * targets // 128) * 128
    spare = lanes - width * targets

    firsts = jnp.arange(stripes, dtype=jnp.int32)[:, None] * stripe
    a_keys = jnp.where(a_live > 0, a_columns, -total).reshape(stripes, width) - firsts
    a_keys = jnp.repeat(a_keys, targets, axis=1)
    a_keys = jnp.pad(a_keys, ((0, 0), (0, spare)), constant_values=-1)[:, None]
    place = jnp.broadcast_to((atom_rows - row * run).reshape(1, 1, 1), (stripes, 1, lanes))
    table = jnp.tile(c_columns[:, 0, :], (1, width))
    table = jnp.pad(table, ((0, 0), (0, spare)), constant_values=-2)
    pack = jnp.concatenate(
        [
            a_keys,
            place,
            jnp.zeros((stripes, 6, lanes), jnp.int32),
            jnp.broadcast_to(table[None], (stripes, run, lanes)),
        ],
        axis=1,
    )
    b_keys = jnp.where(b_live > 0, b_columns, -1).reshape(-1)
    b_rows = jnp.arange(block_count, dtype=jnp.int32) // list_width
    keys = jnp.broadcast_to(jnp.stack([b_keys, b_rows])[:, :, None], (2, block_count, lanes))
    keep = lax.dynamic_slice_in_dim(c_live[:, 0, :], depth * share, share, 1).reshape(-1)

    copies = n_col * len(kinds)
    result = pl.pallas_call(
        functools.partial(kernel, n_row, n_col, n_depth, kinds, slots),
        out_shape=jax.ShapeDtypeStruct((run, share, edge, edge), jnp.bfloat16),
        in_specs=[
            pl.BlockSpec(memory_space=pltpu.VMEM),
            pl.BlockSpec(memory_space=pltpu.VMEM),
            pl.BlockSpec(memory_space=pltpu.SMEM),
            pl.BlockSpec(memory_space=pl.ANY),
            pl.BlockSpec(memory_space=pl.ANY),
        ],
        out_specs=pl.BlockSpec(memory_space=pltpu.VMEM),
        scratch_shapes=[
            pltpu.VMEM((row_count, 8 + run, lanes), jnp.int32),
            pltpu.VMEM((row_count + run, lanes), jnp.int32),
            pltpu.SMEM((row_count + run, lanes), jnp.int32),
            pltpu.VMEM((row_count, width, edge, edge), jnp.bfloat16),
            pltpu.VMEM((block_count + 1, edge, edge), jnp.bfloat16),
            pltpu.VMEM((n_row, n_depth, run, share, edge, edge), jnp.bfloat16),
            pltpu.VMEM((2, run, share, edge, edge), jnp.bfloat16),
            pltpu.VMEM((len(senders), run, share, edge, edge), jnp.bfloat16),
            pltpu.VMEM((run if n_row == 4 else 1, width, edge, edge), jnp.bfloat16),
            pltpu.SemaphoreType.DMA((run,)),
            pltpu.SemaphoreType.DMA,
            pltpu.SemaphoreType.DMA,
            pltpu.SemaphoreType.DMA,
            pltpu.SemaphoreType.DMA,
            pltpu.SemaphoreType.DMA,
            pltpu.SemaphoreType.DMA((copies,)),
            pltpu.SemaphoreType.DMA((row_count,)),
            pltpu.SemaphoreType.DMA((2,)),
            pltpu.SemaphoreType.DMA((2,)),
            pltpu.SemaphoreType.REGULAR,
            pltpu.SemaphoreType.DMA((n_row, n_depth)),
            pltpu.SemaphoreType.DMA((len(senders),)),
        ],
        compiler_params=pltpu.CompilerParams(
            has_side_effects=True, vmem_limit_bytes=60 * 1024 * 1024
        ),
    )(
        pack,
        keys,
        keep,
        a_blocks.reshape(-1, edge, edge),
        b_blocks.reshape(-1, edge, edge),
    )
    return result[:, None]


def solution(mesh):
    placed = (
        P(("row", "col", "depth"), None, None, None, None),
        P(("row", "col", "depth"), None, None),
        P(("row", "col", "depth"), None, None),
        P(("row", "col", "depth")),
        P(("row", "depth"), "col", None, None, None),
        P(("row", "depth"), "col", None),
        P(("row", "depth"), "col", None),
        P("row", "col", None),
        P("row", "col", None),
    )
    return jax.shard_map(
        on_device,
        mesh=mesh,
        in_specs=placed,
        out_specs=P("row", "col", "depth", None, None),
        check_vma=False,
    )
```

```python
import functools

import jax
import jax.numpy as jnp
from jax import lax
from jax.experimental import pallas as pl
from jax.experimental.pallas import tpu as pltpu
from jax.sharding import PartitionSpec as P

GW = 10
REACH = 16
MESH = pl.DeviceIdType.MESH


def stripe_kinds(total, stripe, panel):
    kinds = {}
    for rel in range(total // stripe):
        groups = []
        for g in range(stripe // GW):
            first = rel * stripe + g * GW
            if any((k + REACH) % total < panel + 2 * REACH for k in range(first, first + GW)):
                groups.append(g)
        if groups:
            kinds[rel] = (groups[0], groups[-1] + 1)
    return kinds


def flip(index, step, count):
    return lax.rem(index // 2 + step // 2, count // 2) * 2 + lax.rem(index + step, 2)


def kernel(
    n_row, n_col, n_depth, kinds, slots,
    pack_ref, keys_ref, keep_ref, a_ref, b_ref, out_ref,
    lbuf, picks, pick_s, abuf, bbuf, cbuf, mbuf, pbuf,
    rbuf, r_recv, f_send,
    l_send, l_recv, s_sem, b_sem, a_send, a_recv, m_send, m_recv, m_free, c_send, c_recv,
):
    row, col, depth = (lax.axis_index(name) for name in ("row", "col", "depth"))
    stripes = n_row * n_depth
    per_panel = stripes // n_col
    run = n_col * n_depth
    rows = n_row * run
    me = (row * n_col + col) * n_depth + depth
    my_stripe = row * n_depth + depth
    my_rel = lax.rem(my_stripe - per_panel * col + stripes, stripes)
    rels = sorted(kinds)
    blocks = b_ref.shape[0]
    share = pbuf.shape[2]
    targets = share * n_depth
    width = a_ref.shape[0] // stripes
    groups = width // slots
    active = functools.reduce(jnp.logical_or, [my_rel == rel for rel in rels])
    paired = [rel for rel in rels if rel ^ 1 in kinds and n_depth == 2]
    lone = [rel for rel in rels if rel not in paired]
    senders = sorted({rel // 2 * 2 if rel in paired else rel for rel in rels})

    relayed = (n_row, n_col, n_depth) == (4, 4, 2) and sorted(kinds) == [0, 1, 2, 7]

    def sender(rel):
        return senders.index(rel // 2 * 2 if rel in paired else rel)

    def a_part(ref, rel):
        low, high = kinds[rel]
        return ref.at[pl.ds(low * slots, (high - low) * slots)]

    def list_copy(offset):
        dest = lax.rem(me + offset, rows)
        dest_row, dest_col, dest_depth = dest // run, dest // n_depth % n_col, dest % n_depth
        return pltpu.make_async_remote_copy(
            src_ref=pack_ref.at[dest_row * n_depth + dest_depth],
            dst_ref=lbuf.at[me],
            send_sem=l_send,
            recv_sem=l_recv,
            device_id=(dest_row, dest_col, dest_depth),
            device_id_type=MESH,
        )

    pltpu.make_async_copy(pack_ref.at[my_stripe], lbuf.at[me], l_recv).start()

    def send_list(offset, carry):
        list_copy(offset).start()
        return carry

    lax.fori_loop(1, rows, send_list, 0)

    b_copy = pltpu.make_async_copy(b_ref, bbuf.at[pl.ds(0, blocks)], b_sem)

    @pl.when(active)
    def _():
        b_copy.start()

    sends = []
    for heavy, t in [(h, t) for h in (True, False) for t in reversed(range(n_col))]:
        c = flip(row, t, n_col)
        for rel in [r for r in rels if (r in (0, 1)) == heavy]:
            s = lax.rem(per_panel * c + rel, stripes)
            low, high = kinds[rel]
            src = a_ref.at[pl.ds(s * width + low * slots, (high - low) * slots)]
            if relayed and t == 3 and rel == 1:
                place = col * n_depth + depth
                remote = pltpu.make_async_remote_copy(
                    src_ref=src,
                    dst_ref=rbuf.at[place],
                    send_sem=a_send.at[len(sends)],
                    recv_sem=r_recv.at[place],
                    device_id=(flip(c, 1, n_row), c, 1 - lax.rem(c, 2)),
                    device_id_type=MESH,
                )
                remote.start()
                sends.append((False, remote))
                continue
            mine = (my_stripe == s) & (col == c)
            remote = pltpu.make_async_remote_copy(
                src_ref=src,
                dst_ref=a_part(abuf.at[me], rel),
                send_sem=a_send.at[len(sends)],
                recv_sem=a_recv.at[me],
                device_id=(s // n_depth, c, s % n_depth),
                device_id_type=MESH,
            )
            local = pltpu.make_async_copy(src, a_part(abuf.at[me], rel), a_recv.at[me])
            sends.append((mine, remote))

            @pl.when(mine)
            def _(local=local):
                local.start()

            @pl.when(jnp.logical_not(mine))
            def _(remote=remote):
                remote.start()

    forwards = (row == flip(col, 1, n_row)) & (depth == 1 - lax.rem(col, 2))

    def forward_copy(q):
        p = flip(col, 3, n_row) * run + q
        return pltpu.make_async_remote_copy(
            src_ref=rbuf.at[q],
            dst_ref=abuf.at[p],
            send_sem=f_send,
            recv_sem=a_recv.at[p],
            device_id=(col, col, 1),
            device_id_type=MESH,
        )

    if relayed:

        @pl.when(forwards)
        def _():
            def forward(q, carry):
                pltpu.make_async_copy(rbuf.at[q], rbuf.at[q], r_recv.at[q]).wait()
                forward_copy(q).start()
                return carry

            lax.fori_loop(0, run, forward, 0)

    for rel in rels:
        low, high = kinds[rel]
        gaps = [g for g in range(groups) if not low <= g < high]
        if gaps:

            @pl.when(my_rel == rel)
            def _(gaps=gaps):
                def clear(p, carry):
                    for g in gaps:
                        for v in range(g * slots, (g + 1) * slots):
                            abuf[p, v] = jnp.zeros(abuf.shape[2:], abuf.dtype)
                    return carry

                lax.fori_loop(0, rows, clear, 0)

    pltpu.make_async_copy(lbuf, lbuf, l_recv).wait()
    lanes = lbuf.shape[2]

    def match(p, carry):
        column_row = lbuf[p, 0:1, :]
        place = lbuf[p, 1:2, :]
        table = lbuf[(p // run * n_col + col) * n_depth, 8:, :]
        at = lax.broadcasted_iota(jnp.int32, (run, lanes), 0)
        wanted = jnp.sum(jnp.where(at == place, table, 0), axis=0, keepdims=True)
        hit = (keys_ref[1] == column_row) & (keys_ref[0] == wanted)
        number = lax.broadcasted_iota(jnp.int32, (blocks, lanes), 0)
        picks[pl.ds(p, 1), :] = jnp.min(
            jnp.where(hit, number, blocks), axis=0, keepdims=True
        )
        return carry

    lax.fori_loop(0, rows, match, 0)
    for q in range(run):
        picks[pl.ds(rows + q, 1), :] = lbuf[row * run + q, 1:2, :]
    to_scalars = pltpu.make_async_copy(picks, pick_s, s_sem)
    to_scalars.start()
    to_scalars.wait()

    def share_copy(target_row, d, slot):
        return pltpu.make_async_remote_copy(
            src_ref=cbuf.at[target_row, d],
            dst_ref=pbuf.at[slot],
            send_sem=c_send.at[target_row, d],
            recv_sem=c_recv.at[slot],
            device_id=(target_row, col, d),
            device_id_type=MESH,
        )

    def start_share(target_row, d, slot):
        own = (target_row == row) & (depth == d)

        @pl.when(jnp.logical_not(own))
        def _():
            share_copy(target_row, d, slot).start()

        @pl.when(own)
        def _():
            pltpu.make_async_copy(cbuf.at[target_row, d], pbuf.at[slot], c_recv.at[slot]).start()

    def settle_share(target_row, d):
        @pl.when(jnp.logical_not((target_row == row) & (depth == d)))
        def _():
            share_copy(target_row, d, 0).wait_send()

    is_paired = functools.reduce(jnp.logical_or, [my_rel == rel for rel in paired], False)

    def mate_copy(t, target_row):
        return pltpu.make_async_remote_copy(
            src_ref=cbuf.at[target_row, 1 - depth],
            dst_ref=mbuf.at[t % 2],
            send_sem=m_send.at[t % 2],
            recv_sem=m_recv.at[t % 2],
            device_id=(row, col, 1 - depth),
            device_id_type=MESH,
        )

    @pl.when(active)
    def _():
        b_copy.wait()
        bbuf[blocks] = jnp.zeros(bbuf.shape[1:], bbuf.dtype)

        def one_run(t, carry):
            target_row = flip(col, n_row - 1 - t, n_row)

            def one_row(q, inner):
                p = target_row * run + q
                for rel in rels:

                    @pl.when(my_rel == rel)
                    def _(rel=rel):
                        part = a_part(abuf.at[p], rel)
                        pltpu.make_async_copy(part, part, a_recv.at[p]).wait()

                for u in range(0, targets, 2):
                    total = None
                    for v in range(0, width, 2):
                        left = jnp.concatenate([abuf[p, v], abuf[p, v + 1]], axis=1)
                        right = jnp.concatenate(
                            [
                                jnp.concatenate(
                                    [
                                        bbuf[pick_s[p, (v + i) * targets + u]],
                                        bbuf[pick_s[p, (v + i) * targets + u + 1]],
                                    ],
                                    axis=1,
                                )
                                for i in range(2)
                            ],
                            axis=0,
                        )
                        term = jnp.dot(left, right, preferred_element_type=jnp.float32)
                        total = term if total is None else total + term
                    edge = abuf.shape[-1]
                    for i in range(2):
                        cbuf[target_row, (u + i) // share, q, (u + i) % share] = total[
                            :, i * edge : (i + 1) * edge
                        ].astype(cbuf.dtype)
                return inner

            lax.fori_loop(0, run, one_row, 0)
            for rel in lone:

                @pl.when(my_rel == rel)
                def _(rel=rel):
                    for d in range(n_depth):
                        start_share(target_row, d, sender(rel))

            if paired:

                @pl.when(is_paired)
                def _():
                    @pl.when(t >= 2)
                    def _():
                        pl.semaphore_wait(m_free, 1)

                    exchange = mate_copy(t, target_row)
                    exchange.start()
                    exchange.wait()

                    def merge(q, inner):
                        for u in range(share):
                            cbuf[target_row, depth, q, u] = (
                                cbuf[target_row, depth, q, u].astype(jnp.float32)
                                + mbuf[t % 2, q, u].astype(jnp.float32)
                            ).astype(cbuf.dtype)
                        return inner

                    lax.fori_loop(0, run, merge, 0)

                    @pl.when(t < n_row - 2)
                    def _():
                        pl.semaphore_signal(
                            m_free,
                            inc=1,
                            device_id=(row, col, 1 - depth),
                            device_id_type=MESH,
                        )

                for slot, first in enumerate(senders):
                    if first in paired:

                        @pl.when(my_rel // 2 * 2 == first)
                        def _(slot=slot):
                            start_share(target_row, depth, slot)

            return carry

        lax.fori_loop(0, n_row, one_run, 0)

    for slot in range(len(senders)):
        pltpu.make_async_copy(pbuf.at[slot], pbuf.at[slot], c_recv.at[slot]).wait()

    def finish(i, carry):
        q = jnp.int32(0)
        for j in range(run):
            q = jnp.where(pick_s[rows + j, 0] == i, j, q)
        for u in range(share):
            value = pbuf[0, q, u].astype(jnp.float32)
            for slot in range(1, len(senders)):
                value = value + pbuf[slot, q, u].astype(jnp.float32)
            kept = keep_ref[i * share + u] > 0
            out_ref[i, u] = jnp.where(kept, value, jnp.float32(0.0)).astype(out_ref.dtype)
        return carry

    lax.fori_loop(0, run, finish, 0)

    sent = lbuf.at[pl.ds(0, rows - 1)]
    pltpu.make_async_copy(sent, sent, l_send).wait()
    if relayed:

        @pl.when(forwards)
        def _():
            pltpu.make_async_copy(rbuf, rbuf, f_send).wait()

    for mine, remote in sends:
        if mine is False:
            remote.wait_send()
            continue

        @pl.when(jnp.logical_not(mine))
        def _(remote=remote):
            remote.wait_send()

    def settle(target_row, carry):
        for rel in lone:

            @pl.when(my_rel == rel)
            def _():
                for d in range(n_depth):
                    settle_share(target_row, d)

        if paired:

            @pl.when(is_paired)
            def _():
                settle_share(target_row, depth)

        return carry

    lax.fori_loop(0, n_row, settle, 0)


def on_device(
    a_blocks, a_columns, a_live, atom_rows, b_blocks, b_columns, b_live, c_columns, c_live
):
    n_row, n_col, n_depth = (lax.axis_size(name) for name in ("row", "col", "depth"))
    row, depth = (lax.axis_index(name) for name in ("row", "depth"))
    _, group_count, slots = a_columns.shape
    edge = a_blocks.shape[-1]
    stripe, _, list_width = b_columns.shape
    run, _, targets = c_columns.shape
    stripes = n_row * n_depth
    total = stripe * stripes
    share = targets // n_depth
    width = group_count * slots // stripes
    row_count = n_row * run
    kinds = stripe_kinds(total, stripe, total // n_col)
    senders = {rel // 2 * 2 if rel ^ 1 in kinds and n_depth == 2 else rel for rel in kinds}
    block_count = stripe * list_width
    lanes = -(-width * targets // 128) * 128
    spare = lanes - width * targets

    firsts = jnp.arange(stripes, dtype=jnp.int32)[:, None] * stripe
    a_keys = jnp.where(a_live > 0, a_columns, -total).reshape(stripes, width) - firsts
    a_keys = jnp.repeat(a_keys, targets, axis=1)
    a_keys = jnp.pad(a_keys, ((0, 0), (0, spare)), constant_values=-1)[:, None]
    place = jnp.broadcast_to((atom_rows - row * run).reshape(1, 1, 1), (stripes, 1, lanes))
    table = jnp.tile(c_columns[:, 0, :], (1, width))
    table = jnp.pad(table, ((0, 0), (0, spare)), constant_values=-2)
    pack = jnp.concatenate(
        [
            a_keys,
            place,
            jnp.zeros((stripes, 6, lanes), jnp.int32),
            jnp.broadcast_to(table[None], (stripes, run, lanes)),
        ],
        axis=1,
    )
    b_keys = jnp.where(b_live > 0, b_columns, -1).reshape(-1)
    b_rows = jnp.arange(block_count, dtype=jnp.int32) // list_width
    keys = jnp.broadcast_to(jnp.stack([b_keys, b_rows])[:, :, None], (2, block_count, lanes))
    keep = lax.dynamic_slice_in_dim(c_live[:, 0, :], depth * share, share, 1).reshape(-1)

    copies = n_col * len(kinds)
    result = pl.pallas_call(
        functools.partial(kernel, n_row, n_col, n_depth, kinds, slots),
        out_shape=jax.ShapeDtypeStruct((run, share, edge, edge), jnp.bfloat16),
        in_specs=[
            pl.BlockSpec(memory_space=pltpu.VMEM),
            pl.BlockSpec(memory_space=pltpu.VMEM),
            pl.BlockSpec(memory_space=pltpu.SMEM),
            pl.BlockSpec(memory_space=pl.ANY),
            pl.BlockSpec(memory_space=pl.ANY),
        ],
        out_specs=pl.BlockSpec(memory_space=pltpu.VMEM),
        scratch_shapes=[
            pltpu.VMEM((row_count, 8 + run, lanes), jnp.int32),
            pltpu.VMEM((row_count + run, lanes), jnp.int32),
            pltpu.SMEM((row_count + run, lanes), jnp.int32),
            pltpu.VMEM((row_count, width, edge, edge), jnp.bfloat16),
            pltpu.VMEM((block_count + 1, edge, edge), jnp.bfloat16),
            pltpu.VMEM((n_row, n_depth, run, share, edge, edge), jnp.bfloat16),
            pltpu.VMEM((2, run, share, edge, edge), jnp.bfloat16),
            pltpu.VMEM((len(senders), run, share, edge, edge), jnp.bfloat16),
            pltpu.VMEM((run if n_row == 4 else 1, width, edge, edge), jnp.bfloat16),
            pltpu.SemaphoreType.DMA((run,)),
            pltpu.SemaphoreType.DMA,
            pltpu.SemaphoreType.DMA,
            pltpu.SemaphoreType.DMA,
            pltpu.SemaphoreType.DMA,
            pltpu.SemaphoreType.DMA,
            pltpu.SemaphoreType.DMA((copies,)),
            pltpu.SemaphoreType.DMA((row_count,)),
            pltpu.SemaphoreType.DMA((2,)),
            pltpu.SemaphoreType.DMA((2,)),
            pltpu.SemaphoreType.REGULAR,
            pltpu.SemaphoreType.DMA((n_row, n_depth)),
            pltpu.SemaphoreType.DMA((len(senders),)),
        ],
        compiler_params=pltpu.CompilerParams(
            has_side_effects=True, vmem_limit_bytes=60 * 1024 * 1024
        ),
    )(
        pack,
        keys,
        keep,
        a_blocks.reshape(-1, edge, edge),
        b_blocks.reshape(-1, edge, edge),
    )
    return result[:, None]


def solution(mesh):
    placed = (
        P(("row", "col", "depth"), None, None, None, None),
        P(("row", "col", "depth"), None, None),
        P(("row", "col", "depth"), None, None),
        P(("row", "col", "depth")),
        P(("row", "depth"), "col", None, None, None),
        P(("row", "depth"), "col", None),
        P(("row", "depth"), "col", None),
        P("row", "col", None),
        P("row", "col", None),
    )
    return jax.shard_map(
        on_device,
        mesh=mesh,
        in_specs=placed,
        out_specs=P("row", "col", "depth", None, None),
        check_vma=False,
    )
```
